512 devices in a mesh: aux: 32 (over z, y_hi), pair: 16 (over x, y_lo, core).
Axes of the slice: x: 4, y: 4 (y_hi: 2, y_lo: 2; y = y_hi * 2 + y_lo), z: 16, core: 2. Of those that a mesh axis runs over, the one named last changes fastest.
Arguments:
- integrals: float32 [2048, 16, 320], P('aux', 'pair'), may hold values from -0.6 to 0.6
- metric_root: float32 [2048, 2048], P('aux'), as said below
- occ_energy: float32 [16], replicated, may hold values from -2 to -0.3
- virt_energy: float32 [320], replicated, may hold values from 0.3 to 3
- partner: int32 [1, 16], replicated, may hold values from 0 to 15, as said below
Outputs:
- density: float32 [2048, 16, 320], P('aux', 'pair')
The draws below stay inside these ranges and needn't reach their ends.
Inputs may be any that keep to these rules, and one draw needn't show every extreme that they name: For each r there is one m_r in 1 .. 15 with partner[r, I] = I XOR m_r for every block I; the m_r of different rows differ, so each row is a perfect matching of the blocks. metric_root is symmetric.
All inputs are finite; a program needn't handle non-finite values.
Results may differ from the reference program's by a relative error of at most 0.0003.
Values sent between devices are 32-bit elements; how exact they have to be, the bound alone decides.
A program may use at most 64 MiB of HBM per device.

```python
import math
import jax
import jax.numpy as jnp
from jax import lax

NV = 320
NAUX = 2048
OCC_BLK = 1
ROUNDS = 1
NOCC = 16
N_PAIR = 16


def draw_metric_root(key, part):
    normal_draw = jax.random.normal(key, (NAUX, NAUX), jnp.float32)
    symmetric = (normal_draw + normal_draw.T) * (0.5 / math.sqrt(2.0 * NAUX))
    identity = jnp.eye(NAUX, dtype=jnp.float32)
    return identity + symmetric


def draw_partner(key, part):
    xor_masks = (jax.random.permutation(key, N_PAIR - 1)[:ROUNDS] + 1).astype(jnp.int32)
    block_ids = jnp.arange(N_PAIR, dtype=jnp.int32)
    return jnp.bitwise_xor(block_ids[None, :], xor_masks[:, None]).astype(jnp.int32)


def steps_of(key, dims, cuts, smallest, top_value):
    loudness, own = 1.0, jax.random.fold_in(key, 6)
    for axis_at, shards_of in cuts:
        steps = jnp.exp(jax.random.uniform(jax.random.fold_in(own, axis_at), (shards_of,), jnp.float32, smallest / len(cuts), top_value / len(cuts)))
        loudness = loudness * jnp.repeat(steps, dims[axis_at] // shards_of).reshape([-1 if axis == axis_at else 1 for axis in range(len(dims))])
    return loudness


def noise(own_key, dims, scale, most, cuts=(), kind=jnp.bfloat16):
    factor_of = steps_of(own_key, dims, cuts, -0.22, 0.18) if cuts else 1.0
    result = jax.random.normal(own_key, dims, jnp.float32) * scale * factor_of
    return jnp.minimum(jnp.maximum(result, -most), most).astype(kind)


def setup_inputs(seed: int = 0) -> dict:
    splits = jax.random.split(jax.random.key(seed), 6)
    integrals = noise(splits[0], (NAUX, NOCC, NV), 0.1, 0.6, ((0, 32), (1, 16)), jnp.float32)
    metric_root = draw_metric_root(jax.random.fold_in(splits[5], 71), 0)
    occ_energy = jnp.clip(jax.random.uniform(splits[2], (NOCC,), jnp.float32, -2.0, -0.3), -2.0, -0.3)
    virt_energy = jnp.clip(jax.random.uniform(splits[3], (NV,), jnp.float32, 0.3, 3.0), 0.3, 3.0)
    partner = draw_partner(jax.random.fold_in(splits[5], 71), 0)
    return {"integrals": integrals, "metric_root": metric_root, "occ_energy": occ_energy, "virt_energy": virt_energy, "partner": partner}


highest = lax.Precision.HIGHEST


def pair_sums(own_rows, partner_rows):
    return lax.dot_general(own_rows, partner_rows, (((0,), (0,)), ((), ())), precision=highest, preferred_element_type=jnp.float32)


def combine_amplitudes(summed, own_energy, partner_energy, virt_energy):
    occ_count = own_energy.shape[0]
    vir_count = virt_energy.shape[0]
    occ_pair = own_energy[:, None] + partner_energy[None, :]
    denominator = occ_pair[:, None, :, None] - virt_energy[None, :, None, None] - virt_energy[None, None, None, :]
    amplitudes = summed.reshape(occ_count, vir_count, occ_count, vir_count) / denominator
    combined = 2.0 * amplitudes - jnp.transpose(amplitudes, (0, 3, 2, 1))
    return combined.reshape(occ_count * vir_count, occ_count * vir_count)


def reference(integrals, metric_root, occ_energy, virt_energy, partner):
    row_width = OCC_BLK * NV
    factors = jnp.dot(metric_root, integrals.reshape(NAUX, NOCC * NV), preferred_element_type=jnp.float32, precision=highest)

    def one_block(own_block):
        own_rows = lax.dynamic_slice_in_dim(factors, own_block * row_width, row_width, 1)
        own_energy = lax.dynamic_slice_in_dim(occ_energy, own_block * OCC_BLK, OCC_BLK, 0)
        running = jnp.zeros((NAUX, row_width), jnp.float32)
        other_ids = [own_block] + [partner[round_id, own_block] for round_id in range(ROUNDS)]
        for other_id in other_ids:
            other_id = other_id.astype(jnp.int32)
            partner_rows = lax.dynamic_slice_in_dim(factors, other_id * row_width, row_width, 1)
            partner_energy = lax.dynamic_slice_in_dim(occ_energy, other_id * OCC_BLK, OCC_BLK, 0)
            summed = pair_sums(own_rows, partner_rows)
            combined = combine_amplitudes(summed, own_energy, partner_energy, virt_energy)
            running = running + jnp.dot(partner_rows, combined.T, preferred_element_type=jnp.float32, precision=highest)
        return running

    blocks = lax.map(one_block, jnp.arange(N_PAIR, dtype=jnp.int32))
    return jnp.transpose(blocks, (1, 0, 2)).reshape(NAUX, NOCC, NV)
```

```python
import functools

import jax
import jax.numpy as jnp
from jax import lax
from jax.experimental import pallas as pl
from jax.experimental.pallas import tpu as pltpu
from jax.sharding import PartitionSpec as P

MESH = pl.DeviceIdType.MESH
HIGHEST = lax.Precision.HIGHEST


def flip(index, bit):
    return index + bit - 2 * bit * ((index // bit) % 2)


def dot(left, right, dims):
    return lax.dot_general(
        left, right, (dims, ((), ())), precision=HIGHEST, preferred_element_type=jnp.float32
    )


def kernel(
    nz, bits, cut,
    partner_ref, occ_ref, ints_ref, metric_ref, vrow_ref, vcol_ref, out_ref,
    gat, fac, fj, bf, sums, den, rneg, rpos, ybuf, full, total,
    y_s, y_r, gs, gr, bs, br, ns, nr, ps, pr, y2_s, y2_r, as_, ar,
):
    aux = lax.axis_index("aux")
    pair = lax.axis_index("pair")
    z = aux // 2
    yh = aux % 2
    rows, vir = ints_ref.shape
    up = lax.rem(z + 1, nz) * 2 + yh
    down = lax.rem(z + nz - 1, nz) * 2 + yh
    across = z * 2 + 1 - yh
    half = nz // 2

    barrier = pltpu.get_barrier_semaphore()
    for other in (up, down, across):
        pl.semaphore_signal(barrier, inc=1, device_id={"aux": other, "pair": pair}, device_id_type=MESH)
    for b in range(bits):
        pl.semaphore_signal(barrier, inc=1, device_id={"aux": aux, "pair": flip(pair, 2**b)}, device_id_type=MESH)
    pl.semaphore_wait(barrier, 3 + bits)

    def remote(src, dst, s, r, dev_aux, dev_pair=None):
        return pltpu.make_async_remote_copy(
            src_ref=src, dst_ref=dst, send_sem=s, recv_sem=r,
            device_id={"aux": dev_aux, "pair": pair if dev_pair is None else dev_pair},
            device_id_type=MESH,
        )

    mine = gat.at[z, yh]
    mine[...] = ints_ref[...]
    ycopy = remote(ints_ref, mine, y_s, y_r, across)
    ycopy.start()

    def ring(step, d, h):
        block = lax.rem(z - step + nz, nz) if d == 0 else lax.rem(z + step, nz)
        part = yh if h == 0 else 1 - yh
        ref = gat.at[block, part]
        src = ints_ref if h == 0 and isinstance(step, int) and step == 0 else ref
        return remote(src, ref, gs.at[d, h, step], gr.at[d, h, step], up if d == 0 else down)

    def arrived(step, d):
        return lax.rem(z - step - 1 + nz, nz) if d == 0 else lax.rem(z + step + 1, nz)

    def accumulate(block):
        columns = pl.ds(pl.multiple_of(block * 2 * rows, 2 * rows), 2 * rows)
        fac[...] += dot(metric_ref[:, columns], gat[block].reshape(2 * rows, vir), ((1,), (0,)))

    for d in range(2):
        ring(0, d, 0).start()
    fac[...] = jnp.zeros_like(fac)
    for which in range(2):
        own = occ_ref[pair]
        e = own + own if which == 0 else own + occ_ref[partner_ref[0, pair]]
        den[pl.ds(which * half, half)] = (e - vcol_ref[...] - vrow_ref[...]).reshape(half, cut, vir)
    ycopy.wait()
    for d in range(2):
        ring(0, d, 1).start()
    accumulate(z)

    def gather_step(step, carry):
        for h in range(2):
            for d in range(2):
                ring(step - 1, d, h).wait_recv()
                if d == 0:
                    ring(step, d, h).start()
                else:
                    @pl.when(step < half - 1)
                    def _():
                        ring(step, d, h).start()
        for d in range(2):
            accumulate(arrived(step - 1, d))
        return carry

    lax.fori_loop(1, half, gather_step, 0)
    for h in range(2):
        ring(half - 1, 0, h).wait_recv()
    accumulate(arrived(half - 1, 0))

    def gather_drain(step, carry):
        for h in range(2):
            ring(step, 0, h).wait_send()

            @pl.when(step < half - 1)
            def _():
                ring(step, 1, h).wait_send()
        return carry

    lax.fori_loop(0, half, gather_drain, 0)

    mask = partner_ref[0, 0]
    bf[0] = fac[...]
    for b in range(bits):
        copy = remote(bf.at[2 * b], bf.at[2 * b + 1], bs.at[b], br.at[b], aux, flip(pair, 2**b))
        copy.start()
        if b == 0:
            sums[pl.ds(0, half)] = dot(fac[...], fac[...], ((0,), (0,))).reshape(half, cut, vir)
        copy.wait()
        bit = (mask // 2**b) % 2
        chosen = jnp.where(bit == 1, bf[2 * b + 1], bf[2 * b])
        if b < bits - 1:
            bf[2 * b + 2] = chosen
        else:
            fj[...] = chosen
    sums[pl.ds(half, half)] = dot(fac[...], fj[...], ((0,), (0,))).reshape(half, cut, vir)

    def down_copy(step):
        src = rneg.at[step]
        return remote(src, rneg.at[step + 1], ns.at[step], nr.at[step], down)

    def up_copy(step):
        return remote(rpos.at[step], rpos.at[step + 1], ps.at[step], pr.at[step], up)

    rneg[0] = sums[lax.rem(z - half + nz, nz)]
    rpos[0] = sums[lax.rem(z + half - 1, nz)]
    down_copy(0).start()
    up_copy(0).start()

    def reduce_step(step, carry):
        down_copy(step - 1).wait_recv()
        rneg[step] += sums[lax.rem(z - half + step + nz, nz)]
        down_copy(step).start()
        up_copy(step - 1).wait_recv()
        rpos[step] += sums[lax.rem(z + half - 1 - step, nz)]

        @pl.when(step < half - 1)
        def _():
            up_copy(step).start()
        return carry

    lax.fori_loop(1, half, reduce_step, 0)
    down_copy(half - 1).wait_recv()
    total[...] = rneg[half] + rpos[half - 1]
    y2 = remote(total, ybuf, y2_s, y2_r, across)
    y2.start()
    y2.wait()
    full[z] = (total[...] + ybuf[...]) / den[z]

    def spread(step, d):
        block = lax.rem(z - step + nz, nz) if d == 0 else lax.rem(z + step, nz)
        ref = full.at[block]
        return remote(ref, ref, as_.at[d, step], ar.at[d, step], up if d == 0 else down)

    for d in range(2):
        spread(0, d).start()

    def spread_step(step, carry):
        for d in range(2):
            spread(step - 1, d).wait_recv()
            if d == 0:
                spread(step, d).start()
            else:
                @pl.when(step < half - 1)
                def _():
                    spread(step, d).start()
        return carry

    lax.fori_loop(1, half, spread_step, 0)
    spread(half - 1, 0).wait_recv()

    amp = full[pl.ds(0, half)].reshape(vir, vir)
    cross = full[pl.ds(half, half)].reshape(vir, vir)
    out_ref[...] = (
        dot(fac[...], amp, ((1,), (1,)))
        + 2.0 * dot(fj[...], cross, ((1,), (1,)))
        - dot(fj[...], cross, ((1,), (0,)))
    )

    def drain(step, carry):
        down_copy(step).wait_send()
        spread(step, 0).wait_send()

        @pl.when(step < half - 1)
        def _():
            up_copy(step).wait_send()
            spread(step, 1).wait_send()
        return carry

    lax.fori_loop(0, half, drain, 0)


def shards(nz, integrals, metric_root, occ_energy, virt_energy, partner):
    rows, _, vir = integrals.shape
    bits = 4
    half = nz // 2
    cut = 2 * vir // nz
    vm = pl.BlockSpec(memory_space=pltpu.VMEM)
    sm = pl.BlockSpec(memory_space=pltpu.SMEM)
    f32 = jnp.float32
    dma = pltpu.SemaphoreType.DMA
    out = pl.pallas_call(
        functools.partial(kernel, nz, bits, cut),
        out_shape=jax.ShapeDtypeStruct((rows, vir), f32),
        in_specs=[sm, sm, vm, vm, vm, vm],
        out_specs=vm,
        scratch_shapes=[
            pltpu.VMEM((nz, 2, rows, vir), f32),
            pltpu.VMEM((rows, vir), f32),
            pltpu.VMEM((rows, vir), f32),
            pltpu.VMEM((2 * bits, rows, vir), f32),
            pltpu.VMEM((nz, cut, vir), f32),
            pltpu.VMEM((nz, cut, vir), f32),
            pltpu.VMEM((half + 1, cut, vir), f32),
            pltpu.VMEM((half, cut, vir), f32),
            pltpu.VMEM((cut, vir), f32),
            pltpu.VMEM((nz, cut, vir), f32),
            pltpu.VMEM((cut, vir), f32),
            dma, dma,
            dma((2, 2, half)), dma((2, 2, half)),
            dma((bits,)), dma((bits,)),
            dma((half,)), dma((half,)),
            dma((half,)), dma((half,)),
            dma, dma,
            dma((2, half)), dma((2, half)),
        ],
        compiler_params=pltpu.CompilerParams(collective_id=0, has_side_effects=True),
    )(
        partner, occ_energy, integrals.reshape(rows, vir), metric_root,
        virt_energy.reshape(1, vir), virt_energy.reshape(vir, 1),
    )
    return out.reshape(rows, 1, vir)


def solution(mesh):
    nz = mesh.shape["aux"] // 2
    in_specs = (P("aux", "pair", None), P("aux", None), P(), P(), P())
    return jax.shard_map(
        functools.partial(shards, nz), mesh=mesh, in_specs=in_specs,
        out_specs=P("aux", "pair", None), check_vma=False,
    )
```

```python
import functools

import jax
import jax.numpy as jnp
from jax import lax
from jax.experimental import pallas as pl
from jax.experimental.pallas import tpu as pltpu
from jax.sharding import PartitionSpec as P

MESH = pl.DeviceIdType.MESH
HIGHEST = lax.Precision.HIGHEST


def flip(index, bit):
    return index + bit - 2 * bit * ((index // bit) % 2)


def dot(left, right, dims):
    return lax.dot_general(
        left, right, (dims, ((), ())), precision=HIGHEST, preferred_element_type=jnp.float32
    )


def kernel(
    nz, bits,
    partner_ref, occ_ref, ints_ref, metric_ref, vrow_ref, vcol_ref, out_ref,
    gat, fac, f4, ft4, bf, fj, fjt, fjt4, tq, rb, aq, den, amp,
    y_s, y_r, gs, gr, bs, br, fs, fr, js, jr, rs, rr, cs, cr, ds, dr,
):
    aux = lax.axis_index("aux")
    pair = lax.axis_index("pair")
    z = aux // 2
    yh = aux % 2
    rows, vir = ints_ref.shape
    up = lax.rem(z + 1, nz) * 2 + yh
    down = lax.rem(z + nz - 1, nz) * 2 + yh
    across = z * 2 + 1 - yh
    half = nz // 2
    far = nz // 2
    group = aux // 4
    q = aux % 4
    quarter = vir // 4
    used = quarter * 5 // 2
    part = tq.shape[1] // far
    mates = [group * 4 + lax.rem(q + k, 4) for k in range(1, 4)]
    remotes = [lax.rem(group + k, far) * 4 + q for k in range(1, far)]

    barrier = pltpu.get_barrier_semaphore()
    for other in [up, down] + mates + remotes:
        pl.semaphore_signal(barrier, inc=1, device_id={"aux": other, "pair": pair}, device_id_type=MESH)
    for b in range(bits):
        pl.semaphore_signal(barrier, inc=1, device_id={"aux": aux, "pair": flip(pair, 2**b)}, device_id_type=MESH)
    pl.semaphore_wait(barrier, 4 + far + bits)

    def remote(src, dst, s, r, dev_aux, dev_pair=None):
        return pltpu.make_async_remote_copy(
            src_ref=src, dst_ref=dst, send_sem=s, recv_sem=r,
            device_id={"aux": dev_aux, "pair": pair if dev_pair is None else dev_pair},
            device_id_type=MESH,
        )

    mine = gat.at[z, yh]
    ycopy = remote(ints_ref, mine, y_s, y_r, across)
    ycopy.start()

    def ring(step, d, h):
        block = lax.rem(z - step + nz, nz) if d == 0 else lax.rem(z + step, nz)
        ref = gat.at[block, yh if h == 0 else 1 - yh]
        src = ints_ref if h == 0 and isinstance(step, int) and step == 0 else ref
        return remote(src, ref, gs.at[d, h, step], gr.at[d, h, step], up if d == 0 else down)

    def arrived(step, d):
        return lax.rem(z - step - 1 + nz, nz) if d == 0 else lax.rem(z + step + 1, nz)

    def accumulate(block):
        columns = pl.ds(pl.multiple_of(block * 2 * rows, 2 * rows), 2 * rows)
        fac[...] += dot(metric_ref[:, columns], gat[block].reshape(2 * rows, vir), ((1,), (0,)))

    for d in range(2):
        ring(0, d, 0).start()
    mine[...] = ints_ref[...]
    fac[...] = jnp.zeros_like(fac)
    tq[...] = jnp.zeros_like(tq)
    den[...] = jnp.full(den.shape, -1.0, jnp.float32)
    own_rows = vcol_ref[pl.ds(q * quarter, quarter)]
    short = quarter // 2
    for which in range(2):
        own = occ_ref[pair]
        e = own + own if which == 0 else own + occ_ref[partner_ref[0, pair]]
        for c in range(2):
            den[which, c * quarter:(c + 1) * quarter] = e - own_rows - vrow_ref[:, c * 128:(c + 1) * 128]
        tail = vrow_ref[:, 256:vir]
        den[which, 2 * quarter:used] = jnp.concatenate(
            [e - own_rows[:short] - tail, e - own_rows[short:] - tail], axis=1
        )
    ycopy.wait()
    for d in range(2):
        ring(0, d, 1).start()
    accumulate(z)

    def gather_step(step, carry):
        for h in range(2):
            for d in range(2):
                ring(step - 1, d, h).wait_recv()
                if d == 0:
                    ring(step, d, h).start()
                else:
                    @pl.when(step < half - 1)
                    def _():
                        ring(step, d, h).start()
        for d in range(2):
            accumulate(arrived(step - 1, d))
        return carry

    lax.fori_loop(1, half, gather_step, 0)
    for h in range(2):
        ring(half - 1, 0, h).wait_recv()
    accumulate(arrived(half - 1, 0))

    f_copies = [
        remote(fac, f4.at[q], fs.at[k], fr.at[k], mates[k]) for k in range(3)
    ]
    b_copies = [
        remote(fac if b == 0 else bf.at[2 * b], bf.at[2 * b + 1], bs.at[b], br.at[b], aux, flip(pair, 2**b))
        for b in range(bits)
    ]
    b_copies[0].start()
    for copy in f_copies:
        copy.start()
    f4[q] = fac[...]
    mask = partner_ref[0, 0]

    def choose(b):
        b_copies[b].wait_recv()
        bit = (mask // 2**b) % 2
        kept = fac[...] if b == 0 else bf[2 * b]
        chosen = jnp.where(bit == 1, bf[2 * b + 1], kept)
        if b < bits - 1:
            bf[2 * b + 2] = chosen
            b_copies[b + 1].start()
        else:
            fj[...] = chosen

    def put(h, value):
        for c in range(2):
            tq[h, c * quarter:(c + 1) * quarter] = value[:, c * 128:(c + 1) * 128]
        tq[h, 2 * quarter:used] = jnp.concatenate([value[:short, 256:], value[short:, 256:]], axis=1)

    def piece(u):
        return pl.ds(pl.multiple_of(u * part, 8), part)

    def scatter(h, k):
        to = lax.rem(group + k, far)
        return remote(tq.at[h, piece(to)], rb.at[h, k - 1], rs.at[h, k - 1], rr.at[h, k - 1], remotes[k - 1])

    def reduce(h):
        value = tq[h, piece(group)]
        for k in range(1, far):
            scatter(h, k).wait_recv()
            value = value + rb[h, k - 1]
        aq[h, q, piece(group)] = value / den[h, piece(group)]

    def spread(h, k):
        ref = aq.at[h, q, piece(group)]
        return remote(ref, ref, cs.at[h, k - 1], cr.at[h, k - 1], remotes[k - 1])

    def hand(h, k, m):
        ref = aq.at[h, q, piece(lax.rem(group - k + far, far))]
        return remote(ref, ref, ds.at[h, k, m], dr.at[h, k, m], mates[m])

    order = [k for pair_ in zip(range(1, far // 2 + 1), range(far - 1, far // 2 - 1, -1)) for k in pair_]
    order = list(dict.fromkeys(order))

    for b in range(bits - 1):
        choose(b)
    for m in range(3):
        f_copies[m].wait_recv()
    sum_ii = jnp.zeros((quarter, vir), jnp.float32)
    for src in range(4):
        ft4[src] = f4[src].T
        sum_ii += dot(ft4[src, pl.ds(pl.multiple_of(q * quarter, 8), quarter)], f4[src], ((1,), (0,)))
    put(0, sum_ii)
    for k in order[::-1]:
        scatter(0, k).start()
    choose(bits - 1)
    fjt[...] = fj[...].T
    j_copies = []
    for k in range(3):
        to = lax.rem(q + 1 + k, 4)
        j_copies.append(remote(
            fjt.at[pl.ds(pl.multiple_of(to * quarter, 8), quarter)], fjt4.at[q], js.at[k], jr.at[k], mates[k]
        ))
        j_copies[k].start()
    fjt4[q] = fjt[pl.ds(pl.multiple_of(q * quarter, 8), quarter)]
    for k in range(3):
        j_copies[k].wait_recv()
    sum_ij = jnp.zeros((quarter, vir), jnp.float32)
    for src in range(4):
        sum_ij += dot(fjt4[src], f4[src], ((1,), (0,)))
    put(1, sum_ij)
    for k in order[::-1]:
        scatter(1, k).start()
    for h in range(2):
        reduce(h)
        for k in order[::-1]:
            spread(h, k).start()
        for m in range(3):
            hand(h, 0, m).start()
    for h in range(2):
        for k in order:
            spread(h, k).wait_recv()
            for m in range(3):
                hand(h, k, m).start()
    for h in range(2):
        for k in range(far):
            for m in range(3):
                hand(h, k, m).wait_recv()
        for g in range(4):
            for c in range(2):
                amp[h, g * quarter:(g + 1) * quarter, c * 128:(c + 1) * 128] = (
                    aq[h, g, c * quarter:(c + 1) * quarter]
                )
            for c in range(2):
                amp[h, g * quarter + c * short:g * quarter + (c + 1) * short, 256:vir] = (
                    aq[h, g, 2 * quarter:used, c * 64:(c + 1) * 64]
                )
        if h == 0:
            out_ref[...] = dot(fac[...], amp[0], ((1,), (0,)))
        else:
            out_ref[...] += (
                2.0 * dot(fj[...], amp[1], ((1,), (0,))) - dot(fj[...], amp[1], ((1,), (1,)))
            )

    def gather_drain(step, carry):
        for h in range(2):
            ring(step, 0, h).wait_send()

            @pl.when(step < half - 1)
            def _():
                ring(step, 1, h).wait_send()
        return carry

    lax.fori_loop(0, half, gather_drain, 0)
    for copy in f_copies + b_copies + j_copies:
        copy.wait_send()
    for h in range(2):
        for k in range(1, far):
            scatter(h, k).wait_send()
            spread(h, k).wait_send()
        for k in range(far):
            for m in range(3):
                hand(h, k, m).wait_send()


def shards(nz, integrals, metric_root, occ_energy, virt_energy, partner):
    rows, _, vir = integrals.shape
    bits = 4
    half = nz // 2
    far = nz // 2
    quarter = vir // 4
    padded = -(-(quarter * 5 // 2) // (8 * far)) * 8 * far
    vm = pl.BlockSpec(memory_space=pltpu.VMEM)
    sm = pl.BlockSpec(memory_space=pltpu.SMEM)
    f32 = jnp.float32
    dma = pltpu.SemaphoreType.DMA
    out = pl.pallas_call(
        functools.partial(kernel, nz, bits),
        out_shape=jax.ShapeDtypeStruct((rows, vir), f32),
        in_specs=[sm, sm, vm, vm, vm, vm],
        out_specs=vm,
        scratch_shapes=[
            pltpu.VMEM((nz, 2, rows, vir), f32),
            pltpu.VMEM((rows, vir), f32),
            pltpu.VMEM((4, rows, vir), f32),
            pltpu.VMEM((4, vir, rows), f32),
            pltpu.VMEM((2 * bits, rows, vir), f32),
            pltpu.VMEM((rows, vir), f32),
            pltpu.VMEM((vir, rows), f32),
            pltpu.VMEM((4, quarter, rows), f32),
            pltpu.VMEM((2, padded, 128), f32),
            pltpu.VMEM((2, far - 1, padded // far, 128), f32),
            pltpu.VMEM((2, 4, padded, 128), f32),
            pltpu.VMEM((2, padded, 128), f32),
            pltpu.VMEM((2, vir, vir), f32),
            dma, dma,
            dma((2, 2, half)), dma((2, 2, half)),
            dma((bits,)), dma((bits,)),
            dma((3,)), dma((3,)),
            dma((3,)), dma((3,)),
            dma((2, far - 1)), dma((2, far - 1)),
            dma((2, far - 1)), dma((2, far - 1)),
            dma((2, far, 3)), dma((2, far, 3)),
        ],
        compiler_params=pltpu.CompilerParams(collective_id=0, has_side_effects=True),
    )(
        partner, occ_energy, integrals.reshape(rows, vir), metric_root,
        virt_energy.reshape(1, vir), virt_energy.reshape(vir, 1),
    )
    return out.reshape(rows, 1, vir)


def solution(mesh):
    nz = mesh.shape["aux"] // 2
    in_specs = (P("aux", "pair", None), P("aux", None), P(), P(), P())
    return jax.shard_map(
        functools.partial(shards, nz), mesh=mesh, in_specs=in_specs,
        out_specs=P("aux", "pair", None), check_vma=False,
    )
```

```python
import functools

import jax
import jax.numpy as jnp
from jax import lax
from jax.experimental import pallas as pl
from jax.experimental.pallas import tpu as pltpu
from jax.sharding import PartitionSpec as P

MESH = pl.DeviceIdType.MESH

def flip(index, bit):
    return index + bit - 2 * bit * ((index // bit) % 2)


def split(value):
    high = value.astype(jnp.bfloat16)
    return high, (value - high.astype(jnp.float32)).astype(jnp.bfloat16)


def dot(left, right, dims):
    l_high, l_low = split(left)
    r_high, r_low = split(right)
    one = functools.partial(
        lax.dot_general, dimension_numbers=(dims, ((), ())), preferred_element_type=jnp.float32
    )
    return one(l_high, r_high) + (one(l_high, r_low) + one(l_low, r_high))


def pack(value):
    short = value.shape[0] // 2
    tail = jnp.concatenate([value[:short, 256:], value[short:, 256:]], axis=1)
    return jnp.concatenate([value[:, :128], value[:, 128:256], tail], axis=0)


def unpack(value):
    rows = value.shape[0] * 2 // 5
    tail = jnp.concatenate([value[2 * rows:, :64], value[2 * rows:, 64:]], axis=0)
    return jnp.concatenate([value[:rows], value[rows:2 * rows], tail], axis=1)


def kernel(
    nz, bits,
    partner_ref, occ_ref, ints_ref, metric_ref, virt_ref, out_ref,
    gat, metric2, select, wide, yout, yin, fac, f4p, f4, ft, bf, fj, fjt, fjt4, tq, rb, aq, den, amp, vcol,
    m_s, m_r, y_s, y_r, es, er, os_, or_, bs, br, fs, fr, js, jr, rs, rr, cs, cr, ds, dr,
):
    aux = lax.axis_index("aux")
    pair = lax.axis_index("pair")
    z = aux // 2
    yh = aux % 2
    rows, _, vir = ints_ref.shape
    up = lax.rem(z + 1, nz) * 2 + yh
    down = lax.rem(z + nz - 1, nz) * 2 + yh
    across = z * 2 + 1 - yh
    half = nz // 2
    far = nz // 2
    group = aux // 4
    q = aux % 4
    quarter = vir // 4
    used = quarter * 5 // 2
    part = tq.shape[1] // far
    mates = [group * 4 + lax.rem(q + k, 4) for k in range(1, 4)]
    remotes = [lax.rem(group + k, far) * 4 + q for k in range(1, far)]

    barrier = pltpu.get_barrier_semaphore()
    for other in [up, down] + mates + remotes:
        pl.semaphore_signal(barrier, inc=1, device_id={"aux": other, "pair": pair}, device_id_type=MESH)
    for b in range(bits):
        pl.semaphore_signal(barrier, inc=1, device_id={"aux": aux, "pair": flip(pair, 2**b)}, device_id_type=MESH)
    pl.semaphore_wait(barrier, 4 + far + bits)

    def remote(src, dst, s, r, dev_aux, dev_pair=None):
        return pltpu.make_async_remote_copy(
            src_ref=src, dst_ref=dst, send_sem=s, recv_sem=r,
            device_id={"aux": dev_aux, "pair": pair if dev_pair is None else dev_pair},
            device_id_type=MESH,
        )

    m_copy = remote(metric_ref, metric2, m_s, m_r, across)
    gat[z] = pack(ints_ref[:, 0, :])

    def relay(d, k):
        block = lax.rem(z - 2 * k + 2 * nz, nz) if d == 0 else lax.rem(z + 2 * k, nz)
        ref = gat.at[block]
        if k == half // 2 - 1:
            size = gat.shape[1] // 2
            ref = gat.at[block, pl.ds(d * size, size)]
        return remote(ref, ref, es.at[d, k], er.at[d, k], remotes[0] if d == 0 else remotes[-1])

    def side(d, k):
        block = lax.rem(z - 2 * k + 2 * nz, nz) if d == 0 else lax.rem(z + 2 * k, nz)
        ref = gat.at[block]
        return remote(ref, ref, os_.at[d, k], or_.at[d, k], up if d == 0 else down)

    steps = half // 2
    for d in range(2):
        relay(d, 0).start()
    for d in range(2):
        side(d, 0).start()
    m_copy.start()

    def choose_columns(ref, base):
        for b in range(nz):
            both = ref[:, b * 2 * rows:(b + 1) * 2 * rows]
            select[b, base:base + rows] = jnp.where(yh == 0, both[:, :rows], both[:, rows:])

    choose_columns(metric_ref, 0)
    wide[...] = jnp.zeros_like(wide)
    tq[...] = jnp.zeros_like(tq)
    den[...] = jnp.full(den.shape, -1.0, jnp.float32)
    v_row = virt_ref[...].reshape(1, vir)
    vcol[...] = jnp.broadcast_to(v_row, (8, vir)).T
    own_rows = vcol[pl.ds(pl.multiple_of(q * quarter, 8), quarter), :1]
    short = quarter // 2
    for which in range(2):
        own = occ_ref[pair]
        e = own + own if which == 0 else own + occ_ref[partner_ref[0, pair]]
        den[which, :used] = pack(e - own_rows - v_row)

    for k in range(1, steps):
        for d in range(2):
            relay(d, k - 1).wait_recv()
            relay(d, k).start()
        for d in range(2):
            side(d, k).start()

    def accumulate(block):
        wide[...] += dot(select[block], unpack(gat[block]), ((1,), (0,)))

    m_copy.wait_recv()
    choose_columns(metric2, rows)
    accumulate(z)
    for k in range(steps):
        for d in range(2):
            side(d, k).wait_recv()
            away = 2 * k + 1
            accumulate(lax.rem(z - away + nz, nz) if d == 0 else lax.rem(z + away, nz))
        if k < steps - 1:
            for d in range(2):
                away = 2 * k + 2
                accumulate(lax.rem(z - away + nz, nz) if d == 0 else lax.rem(z + away, nz))
    for d in range(2):
        relay(d, steps - 1).wait_recv()
    accumulate(lax.rem(z + half, nz))
    yout[...] = pack(wide[rows:])
    y_copy = remote(yout, yin, y_s, y_r, across)
    y_copy.start()
    y_copy.wait_recv()
    fac[...] = wide[:rows] + unpack(yin[...])
    bf[0] = pack(fac[...])

    f_copies = [
        remote(bf.at[0], f4p.at[q], fs.at[k], fr.at[k], mates[k]) for k in range(3)
    ]
    b_copies = [
        remote(bf.at[2 * b], bf.at[2 * b + 1], bs.at[b], br.at[b], aux, flip(pair, 2**b))
        for b in range(bits)
    ]
    b_copies[0].start()
    for copy in f_copies:
        copy.start()
    f4p[q] = bf[0]
    mask = partner_ref[0, 0]

    def choose(b):
        b_copies[b].wait_recv()
        bit = (mask // 2**b) % 2
        chosen = jnp.where(bit == 1, bf[2 * b + 1], bf[2 * b])
        if b < bits - 1:
            bf[2 * b + 2] = chosen
            b_copies[b + 1].start()
        else:
            fj[...] = unpack(chosen)

    def put(h, value):
        tq[h, :used] = pack(value)

    def piece(u):
        return pl.ds(pl.multiple_of(u * part, 8), part)

    def scatter(h, k):
        to = lax.rem(group + k, far)
        return remote(tq.at[h, piece(to)], rb.at[h, k - 1], rs.at[h, k - 1], rr.at[h, k - 1], remotes[k - 1])

    def reduce(h):
        value = tq[h, piece(group)]
        for k in range(1, far):
            scatter(h, k).wait_recv()
            value = value + rb[h, k - 1]
        aq[h, q, piece(group)] = value / den[h, piece(group)]

    def spread(h, k):
        ref = aq.at[h, q, piece(group)]
        return remote(ref, ref, cs.at[h, k - 1], cr.at[h, k - 1], remotes[k - 1])

    def hand(h, k, m):
        ref = aq.at[h, q, piece(lax.rem(group - k + far, far))]
        return remote(ref, ref, ds.at[h, k, m], dr.at[h, k, m], mates[m])

    order = [k for pair_ in zip(range(1, far // 2 + 1), range(far - 1, far // 2 - 1, -1)) for k in pair_]
    order = list(dict.fromkeys(order))

    for b in range(bits - 1):
        choose(b)
    for m in range(3):
        f_copies[m].wait_recv()
    for src in range(4):
        f4[src * rows:(src + 1) * rows] = unpack(f4p[src])
    ft[...] = f4[...].T
    own_quarter = pl.ds(pl.multiple_of(q * quarter, 8), quarter)
    sum_ii = dot(ft[own_quarter], f4[...], ((1,), (0,)))
    put(0, sum_ii)
    for k in order[::-1]:
        scatter(0, k).start()
    choose(bits - 1)
    fjt[...] = fj[...].T
    j_copies = []
    for k in range(3):
        to = lax.rem(q + 1 + k, 4)
        j_copies.append(remote(
            fjt.at[pl.ds(pl.multiple_of(to * quarter, 8), quarter)], fjt4.at[q], js.at[k], jr.at[k], mates[k]
        ))
        j_copies[k].start()
    fjt4[q] = fjt[pl.ds(pl.multiple_of(q * quarter, 8), quarter)]
    for k in range(3):
        j_copies[k].wait_recv()
    partner_t = jnp.concatenate([fjt4[src] for src in range(4)], axis=1)
    sum_ij = dot(partner_t, f4[...], ((1,), (0,)))
    put(1, sum_ij)
    for k in order[::-1]:
        scatter(1, k).start()
    for h in range(2):
        reduce(h)
        for k in order[::-1]:
            spread(h, k).start()
        for m in range(3):
            hand(h, 0, m).start()
    for h in range(2):
        for k in order:
            spread(h, k).wait_recv()
            for m in range(3):
                hand(h, k, m).start()
    for h in range(2):
        for k in range(far):
            for m in range(3):
                hand(h, k, m).wait_recv()
        for g in range(4):
            amp[h, g * quarter:(g + 1) * quarter] = unpack(aq[h, g, :used])
        if h == 0:
            first = dot(fac[...], amp[0], ((1,), (0,)))
        else:
            out_ref[:, 0, :] = first + (
                2.0 * dot(fj[...], amp[1], ((1,), (0,))) - dot(fj[...], amp[1], ((1,), (1,)))
            )

    for d in range(2):
        for k in range(steps):
            relay(d, k).wait_send()
            side(d, k).wait_send()
    for copy in [m_copy, y_copy] + f_copies + b_copies + j_copies:
        copy.wait_send()
    for h in range(2):
        for k in range(1, far):
            scatter(h, k).wait_send()
            spread(h, k).wait_send()
        for k in range(far):
            for m in range(3):
                hand(h, k, m).wait_send()


def shards(nz, integrals, metric_root, occ_energy, virt_energy, partner):
    rows, _, vir = integrals.shape
    bits = 4
    half = nz // 2
    far = nz // 2
    quarter = vir // 4
    packed = rows * 5 // 2
    padded = -(-(quarter * 5 // 2) // (8 * far)) * 8 * far
    vm = pl.BlockSpec(memory_space=pltpu.VMEM)
    sm = pl.BlockSpec(memory_space=pltpu.SMEM)
    f32 = jnp.float32
    dma = pltpu.SemaphoreType.DMA
    out = pl.pallas_call(
        functools.partial(kernel, nz, bits),
        out_shape=jax.ShapeDtypeStruct((rows, 1, vir), f32),
        in_specs=[sm, sm, vm, vm, vm],
        out_specs=vm,
        scratch_shapes=[
            pltpu.VMEM((nz, packed, 128), f32),
            pltpu.VMEM(metric_root.shape, f32),
            pltpu.VMEM((nz, 2 * rows, rows), f32),
            pltpu.VMEM((2 * rows, vir), f32),
            pltpu.VMEM((packed, 128), f32),
            pltpu.VMEM((packed, 128), f32),
            pltpu.VMEM((rows, vir), f32),
            pltpu.VMEM((4, packed, 128), f32),
            pltpu.VMEM((4 * rows, vir), f32),
            pltpu.VMEM((vir, 4 * rows), f32),
            pltpu.VMEM((2 * bits, packed, 128), f32),
            pltpu.VMEM((rows, vir), f32),
            pltpu.VMEM((vir, rows), f32),
            pltpu.VMEM((4, quarter, rows), f32),
            pltpu.VMEM((2, padded, 128), f32),
            pltpu.VMEM((2, far - 1, padded // far, 128), f32),
            pltpu.VMEM((2, 4, padded, 128), f32),
            pltpu.VMEM((2, padded, 128), f32),
            pltpu.VMEM((2, vir, vir), f32),
            pltpu.VMEM((vir, 8), f32),
            dma, dma,
            dma, dma,
            dma((2, half // 2)), dma((2, half // 2)),
            dma((2, half // 2)), dma((2, half // 2)),
            dma((bits,)), dma((bits,)),
            dma((3,)), dma((3,)),
            dma((3,)), dma((3,)),
            dma((2, far - 1)), dma((2, far - 1)),
            dma((2, far - 1)), dma((2, far - 1)),
            dma((2, far, 3)), dma((2, far, 3)),
        ],
        compiler_params=pltpu.CompilerParams(collective_id=0, has_side_effects=True),
    )(
        partner, occ_energy, integrals, metric_root, virt_energy,
    )
    return out


def solution(mesh):
    nz = mesh.shape["aux"] // 2
    in_specs = (P("aux", "pair", None), P("aux", None), P(), P(), P())
    return jax.shard_map(
        functools.partial(shards, nz), mesh=mesh, in_specs=in_specs,
        out_specs=P("aux", "pair", None), check_vma=False,
    )
```

```python
import functools

import jax
import jax.numpy as jnp
from jax import lax
from jax.experimental import pallas as pl
from jax.experimental.pallas import tpu as pltpu
from jax.sharding import PartitionSpec as P

MESH = pl.DeviceIdType.MESH

def flip(index, bit):
    return index + bit - 2 * bit * ((index // bit) % 2)


def split(value):
    high = value.astype(jnp.bfloat16)
    return high, (value - high.astype(jnp.float32)).astype(jnp.bfloat16)


def dot(left, right, dims):
    l_high, l_low = split(left)
    r_high, r_low = split(right)
    one = functools.partial(
        lax.dot_general, dimension_numbers=(dims, ((), ())), preferred_element_type=jnp.float32
    )
    return one(l_high, r_high) + (one(l_high, r_low) + one(l_low, r_high))


def pack(value):
    short = value.shape[0] // 2
    tail = jnp.concatenate([value[:short, 256:], value[short:, 256:]], axis=1)
    return jnp.concatenate([value[:, :128], value[:, 128:256], tail], axis=0)


def unpack(value):
    rows = value.shape[0] * 2 // 5
    tail = jnp.concatenate([value[2 * rows:, :64], value[2 * rows:, 64:]], axis=0)
    return jnp.concatenate([value[:rows], value[rows:2 * rows], tail], axis=1)


def kernel(
    nz, bits,
    partner_ref, occ_ref, ints_ref, metric_ref, virt_ref, out_ref,
    gat, metric2, select, wide, yout, yin, f4p, f4, ft, bf, j4p, j4, jt, tq, rb, aq, den, part, pout, pin, vcol,
    m_s, m_r, y_s, y_r, es, er, os_, or_, bs, br, fs, fr, js, jr, rs, rr, cs, cr, ps, pr,
):
    aux = lax.axis_index("aux")
    pair = lax.axis_index("pair")
    z = aux // 2
    yh = aux % 2
    rows, _, vir = ints_ref.shape
    up = lax.rem(z + 1, nz) * 2 + yh
    down = lax.rem(z + nz - 1, nz) * 2 + yh
    across = z * 2 + 1 - yh
    half = nz // 2
    far = nz // 2
    group = aux // 4
    q = aux % 4
    quarter = vir // 4
    used = quarter * 5 // 2
    span = tq.shape[1] // far
    mates = [group * 4 + lax.rem(q + k, 4) for k in range(1, 4)]
    remotes = [lax.rem(group + k, far) * 4 + q for k in range(1, far)]

    barrier = pltpu.get_barrier_semaphore()
    for other in [up, down] + mates + remotes:
        pl.semaphore_signal(barrier, inc=1, device_id={"aux": other, "pair": pair}, device_id_type=MESH)
    for b in range(bits):
        pl.semaphore_signal(barrier, inc=1, device_id={"aux": aux, "pair": flip(pair, 2**b)}, device_id_type=MESH)
    pl.semaphore_wait(barrier, 4 + far + bits)

    def remote(src, dst, s, r, dev_aux, dev_pair=None):
        return pltpu.make_async_remote_copy(
            src_ref=src, dst_ref=dst, send_sem=s, recv_sem=r,
            device_id={"aux": dev_aux, "pair": pair if dev_pair is None else dev_pair},
            device_id_type=MESH,
        )

    m_copy = remote(metric_ref, metric2, m_s, m_r, across)
    gat[z] = pack(ints_ref[:, 0, :])

    def relay(d, k):
        block = lax.rem(z - 2 * k + 2 * nz, nz) if d == 0 else lax.rem(z + 2 * k, nz)
        ref = gat.at[block]
        if k == half // 2 - 1:
            size = gat.shape[1] // 2
            ref = gat.at[block, pl.ds(d * size, size)]
        return remote(ref, ref, es.at[d, k], er.at[d, k], remotes[0] if d == 0 else remotes[-1])

    def side(d, k):
        block = lax.rem(z - 2 * k + 2 * nz, nz) if d == 0 else lax.rem(z + 2 * k, nz)
        ref = gat.at[block]
        return remote(ref, ref, os_.at[d, k], or_.at[d, k], up if d == 0 else down)

    steps = half // 2
    for d in range(2):
        relay(d, 0).start()
    for d in range(2):
        side(d, 0).start()
    m_copy.start()

    def choose_columns(ref, base):
        for b in range(nz):
            both = ref[:, b * 2 * rows:(b + 1) * 2 * rows]
            select[b, base:base + rows] = jnp.where(yh == 0, both[:, :rows], both[:, rows:])

    choose_columns(metric_ref, 0)
    wide[...] = jnp.zeros_like(wide)
    tq[...] = jnp.zeros_like(tq)
    den[...] = jnp.full(den.shape, -1.0, jnp.float32)
    v_row = virt_ref[...].reshape(1, vir)
    vcol[...] = jnp.broadcast_to(v_row, (8, vir)).T
    own_rows = vcol[pl.ds(pl.multiple_of(q * quarter, 8), quarter), :1]
    short = quarter // 2
    for which in range(2):
        own = occ_ref[pair]
        e = own + own if which == 0 else own + occ_ref[partner_ref[0, pair]]
        den[which, :used] = pack(e - own_rows - v_row)

    for k in range(1, steps):
        for d in range(2):
            relay(d, k - 1).wait_recv()
            relay(d, k).start()
        for d in range(2):
            side(d, k).start()

    def accumulate(block):
        wide[...] += dot(select[block], unpack(gat[block]), ((1,), (0,)))

    m_copy.wait_recv()
    choose_columns(metric2, rows)
    accumulate(z)
    for k in range(steps):
        for d in range(2):
            side(d, k).wait_recv()
            away = 2 * k + 1
            accumulate(lax.rem(z - away + nz, nz) if d == 0 else lax.rem(z + away, nz))
        if k < steps - 1:
            for d in range(2):
                away = 2 * k + 2
                accumulate(lax.rem(z - away + nz, nz) if d == 0 else lax.rem(z + away, nz))
    for d in range(2):
        relay(d, steps - 1).wait_recv()
    accumulate(lax.rem(z + half, nz))
    yout[...] = pack(wide[rows:])
    y_copy = remote(yout, yin, y_s, y_r, across)
    y_copy.start()
    y_copy.wait_recv()
    bf[0] = pack(wide[:rows]) + yin[...]

    f_copies = [
        remote(bf.at[0], f4p.at[q], fs.at[k], fr.at[k], mates[k]) for k in range(3)
    ]
    b_copies = [
        remote(bf.at[2 * b], bf.at[2 * b + 1], bs.at[b], br.at[b], aux, flip(pair, 2**b))
        for b in range(bits)
    ]
    b_copies[0].start()
    for copy in f_copies:
        copy.start()
    f4p[q] = bf[0]
    mask = partner_ref[0, 0]

    def choose(b):
        b_copies[b].wait_recv()
        bit = (mask // 2**b) % 2
        chosen = jnp.where(bit == 1, bf[2 * b + 1], bf[2 * b])
        bf[2 * b + 2] = chosen
        if b < bits - 1:
            b_copies[b + 1].start()

    def put(h, value):
        tq[h, :used] = pack(value)

    def piece(u):
        return pl.ds(pl.multiple_of(u * span, 8), span)

    def scatter(h, k):
        to = lax.rem(group + k, far)
        return remote(tq.at[h, piece(to)], rb.at[h, k - 1], rs.at[h, k - 1], rr.at[h, k - 1], remotes[k - 1])

    def reduce(h):
        value = tq[h, piece(group)]
        for k in range(1, far):
            scatter(h, k).wait_recv()
            value = value + rb[h, k - 1]
        aq[h, piece(group)] = value / den[h, piece(group)]

    def spread(h, k):
        ref = aq.at[h, piece(group)]
        return remote(ref, ref, cs.at[h, k - 1], cr.at[h, k - 1], remotes[k - 1])

    order = [k for pair_ in zip(range(1, far // 2 + 1), range(far - 1, far // 2 - 1, -1)) for k in pair_]
    order = list(dict.fromkeys(order))

    for b in range(bits - 1):
        choose(b)
    for m in range(3):
        f_copies[m].wait_recv()
    for src in range(4):
        f4[src * rows:(src + 1) * rows] = unpack(f4p[src])
    ft[...] = f4[...].T
    own_quarter = pl.ds(pl.multiple_of(q * quarter, 8), quarter)
    sum_ii = dot(ft[own_quarter], f4[...], ((1,), (0,)))
    put(0, sum_ii)
    for k in order[::-1]:
        scatter(0, k).start()
    choose(bits - 1)
    j_copies = [remote(bf.at[2 * bits], j4p.at[q], js.at[k], jr.at[k], mates[k]) for k in range(3)]
    for copy in j_copies:
        copy.start()
    j4p[q] = bf[2 * bits]
    for copy in j_copies:
        copy.wait_recv()
    for src in range(4):
        j4[src * rows:(src + 1) * rows] = unpack(j4p[src])
    jt[...] = j4[...].T
    sum_ij = dot(jt[own_quarter], f4[...], ((1,), (0,)))
    put(1, sum_ij)
    for k in order[::-1]:
        scatter(1, k).start()
    for h in range(2):
        reduce(h)
        for k in order[::-1]:
            spread(h, k).start()
    for k in order:
        spread(0, k).wait_recv()
    part[...] = dot(ft[own_quarter], unpack(aq[0, :used]), ((0,), (0,)))
    for k in order:
        spread(1, k).wait_recv()
    cross = unpack(aq[1, :used])
    part[...] += dot(2.0 * jt[own_quarter], cross, ((0,), (0,)))
    swapped = dot(j4[...], cross, ((1,), (1,)))
    for g in range(4):
        @pl.when(q == g)
        def _():
            part[:, g * quarter:(g + 1) * quarter] -= swapped
    p_copies = []
    for k in range(3):
        to = lax.rem(q + 1 + k, 4)
        pout[k] = pack(part[pl.ds(pl.multiple_of(to * rows, 8), rows)])
        p_copies.append(remote(pout.at[k], pin.at[k], ps.at[k], pr.at[k], mates[k]))
        p_copies[k].start()
    total = pack(part[pl.ds(pl.multiple_of(q * rows, 8), rows)])
    for k in range(3):
        p_copies[k].wait_recv()
        total += pin[k]
    out_ref[:, 0, :] = unpack(total)

    for d in range(2):
        for k in range(steps):
            relay(d, k).wait_send()
            side(d, k).wait_send()
    for copy in [m_copy, y_copy] + f_copies + b_copies + j_copies + p_copies:
        copy.wait_send()
    for h in range(2):
        for k in range(1, far):
            scatter(h, k).wait_send()
            spread(h, k).wait_send()


def shards(nz, integrals, metric_root, occ_energy, virt_energy, partner):
    rows, _, vir = integrals.shape
    bits = 4
    half = nz // 2
    far = nz // 2
    quarter = vir // 4
    packed = rows * 5 // 2
    padded = -(-(quarter * 5 // 2) // (8 * far)) * 8 * far
    vm = pl.BlockSpec(memory_space=pltpu.VMEM)
    sm = pl.BlockSpec(memory_space=pltpu.SMEM)
    f32 = jnp.float32
    dma = pltpu.SemaphoreType.DMA
    out = pl.pallas_call(
        functools.partial(kernel, nz, bits),
        out_shape=jax.ShapeDtypeStruct((rows, 1, vir), f32),
        in_specs=[sm, sm, vm, vm, vm],
        out_specs=vm,
        scratch_shapes=[
            pltpu.VMEM((nz, packed, 128), f32),
            pltpu.VMEM(metric_root.shape, f32),
            pltpu.VMEM((nz, 2 * rows, rows), f32),
            pltpu.VMEM((2 * rows, vir), f32),
            pltpu.VMEM((packed, 128), f32),
            pltpu.VMEM((packed, 128), f32),
            pltpu.VMEM((4, packed, 128), f32),
            pltpu.VMEM((4 * rows, vir), f32),
            pltpu.VMEM((vir, 4 * rows), f32),
            pltpu.VMEM((2 * bits + 1, packed, 128), f32),
            pltpu.VMEM((4, packed, 128), f32),
            pltpu.VMEM((4 * rows, vir), f32),
            pltpu.VMEM((vir, 4 * rows), f32),
            pltpu.VMEM((2, padded, 128), f32),
            pltpu.VMEM((2, far - 1, padded // far, 128), f32),
            pltpu.VMEM((2, padded, 128), f32),
            pltpu.VMEM((2, padded, 128), f32),
            pltpu.VMEM((4 * rows, vir), f32),
            pltpu.VMEM((3, packed, 128), f32),
            pltpu.VMEM((3, packed, 128), f32),
            pltpu.VMEM((vir, 8), f32),
            dma, dma,
            dma, dma,
            dma((2, half // 2)), dma((2, half // 2)),
            dma((2, half // 2)), dma((2, half // 2)),
            dma((bits,)), dma((bits,)),
            dma((3,)), dma((3,)),
            dma((3,)), dma((3,)),
            dma((2, far - 1)), dma((2, far - 1)),
            dma((2, far - 1)), dma((2, far - 1)),
            dma((3,)), dma((3,)),
        ],
        compiler_params=pltpu.CompilerParams(collective_id=0, has_side_effects=True),
    )(
        partner, occ_energy, integrals, metric_root, virt_energy,
    )
    return out


def solution(mesh):
    nz = mesh.shape["aux"] // 2
    in_specs = (P("aux", "pair", None), P("aux", None), P(), P(), P())
    return jax.shard_map(
        functools.partial(shards, nz), mesh=mesh, in_specs=in_specs,
        out_specs=P("aux", "pair", None), check_vma=False,
    )
```

```python
import functools

import jax
import jax.numpy as jnp
from jax import lax
from jax.experimental import pallas as pl
from jax.experimental.pallas import tpu as pltpu
from jax.sharding import PartitionSpec as P

MESH = pl.DeviceIdType.MESH

def flip(index, mask):
    for bit in (1, 2, 4, 8):
        if mask & bit:
            index = index + bit - 2 * bit * ((index // bit) % 2)
    return index


def split(value):
    high = value.astype(jnp.bfloat16)
    return high, (value - high.astype(jnp.float32)).astype(jnp.bfloat16)


def dot(left, right, dims):
    l_high, l_low = split(left)
    r_high, r_low = split(right)
    one = functools.partial(
        lax.dot_general, dimension_numbers=(dims, ((), ())), preferred_element_type=jnp.float32
    )
    return one(l_high, r_high) + (one(l_high, r_low) + one(l_low, r_high))


def pack(value):
    short = value.shape[0] // 2
    tail = jnp.concatenate([value[:short, 256:], value[short:, 256:]], axis=1)
    return jnp.concatenate([value[:, :128], value[:, 128:256], tail], axis=0)


def unpack(value):
    rows = value.shape[0] * 2 // 5
    tail = jnp.concatenate([value[2 * rows:, :64], value[2 * rows:, 64:]], axis=0)
    return jnp.concatenate([value[:rows], value[rows:2 * rows], tail], axis=1)


def kernel(
    nz, mask,
    occ_ref, ints_ref, metric_ref, virt_ref, out_ref,
    gat, metric2, select, wide, yout, yin, x4p, x4, xt, bf, tq, rb, aq, den, part, pout, pin, vcol,
    m_s, m_r, y_s, y_r, es, er, os_, or_, bs, br, xs, xr, rs, rr, cs, cr, ps, pr,
):
    aux = lax.axis_index("aux")
    pair = lax.axis_index("pair")
    z = aux // 2
    yh = aux % 2
    rows, _, vir = ints_ref.shape
    up = lax.rem(z + 1, nz) * 2 + yh
    down = lax.rem(z + nz - 1, nz) * 2 + yh
    across = z * 2 + 1 - yh
    half = nz // 2
    far = nz // 2
    group = aux // 4
    q = aux % 4
    quarter = vir // 4
    used = quarter * 5 // 2
    span = tq.shape[1] // far
    mate = lambda k: group * 4 + lax.rem(q + k, 4)
    distant = lambda k: lax.rem(group + k, far) * 4 + q

    barrier = pltpu.get_barrier_semaphore()
    for other in [up, down] + [mate(k) for k in range(1, 4)] + [distant(k) for k in range(1, far)]:
        pl.semaphore_signal(barrier, inc=1, device_id={"aux": other, "pair": pair}, device_id_type=MESH)
    other_pair = flip(pair, mask)
    pl.semaphore_signal(barrier, inc=1, device_id={"aux": aux, "pair": other_pair}, device_id_type=MESH)
    pl.semaphore_wait(barrier, 5 + far)

    def remote(src, dst, s, r, dev_aux, dev_pair=None):
        return pltpu.make_async_remote_copy(
            src_ref=src, dst_ref=dst, send_sem=s, recv_sem=r,
            device_id={"aux": dev_aux, "pair": pair if dev_pair is None else dev_pair},
            device_id_type=MESH,
        )

    m_copy = remote(metric_ref, metric2, m_s, m_r, across)
    gat[z] = pack(ints_ref[:, 0, :])

    def relay(d, k):
        block = lax.rem(z - 2 * k + 2 * nz, nz) if d == 0 else lax.rem(z + 2 * k, nz)
        ref = gat.at[block]
        if k == half // 2 - 1:
            size = gat.shape[1] // 2
            ref = gat.at[block, pl.ds(d * size, size)]
        return remote(ref, ref, es.at[d, k], er.at[d, k], distant(1) if d == 0 else distant(far - 1))

    def side(d, k):
        block = lax.rem(z - 2 * k + 2 * nz, nz) if d == 0 else lax.rem(z + 2 * k, nz)
        ref = gat.at[block]
        return remote(ref, ref, os_.at[d, k], or_.at[d, k], up if d == 0 else down)

    steps = half // 2
    for d in range(2):
        relay(d, 0).start()
    for d in range(2):
        side(d, 0).start()
    m_copy.start()

    def choose_columns(ref, base):
        def one(b, carry):
            both = ref[:, pl.ds(pl.multiple_of(b * 2 * rows, 2 * rows), 2 * rows)]
            select[b, base:base + rows] = jnp.where(yh == 0, both[:, :rows], both[:, rows:])
            return carry

        lax.fori_loop(0, nz, one, 0)

    choose_columns(metric_ref, 0)
    wide[...] = jnp.zeros_like(wide)
    tq[...] = jnp.zeros_like(tq)
    den[...] = jnp.full(den.shape, -1.0, jnp.float32)
    v_row = virt_ref[...].reshape(1, vir)
    vcol[...] = jnp.broadcast_to(v_row, (8, vir)).T
    own_rows = vcol[pl.ds(pl.multiple_of(q * quarter, 8), quarter), :1]
    short = quarter // 2
    for which in range(2):
        own = occ_ref[pair]
        e = own + own if which == 0 else own + occ_ref[other_pair]
        den[which, :used] = pack(e - own_rows - v_row)

    for k in range(1, steps):
        for d in range(2):
            relay(d, k - 1).wait_recv()
            relay(d, k).start()
        for d in range(2):
            side(d, k).start()

    def accumulate(block):
        wide[...] += dot(select[block], unpack(gat[block]), ((1,), (0,)))

    m_copy.wait_recv()
    choose_columns(metric2, rows)

    def near(i, carry):
        accumulate(lax.rem(z + i, nz))
        return carry

    for d in range(2):
        for k in range(steps - 1):
            side(d, k).wait_recv()
    lax.fori_loop(half + 2, 2 * nz - half - 1, near, 0)
    for d in range(2):
        side(d, steps - 1).wait_recv()
    for d in range(2):
        relay(d, steps - 1).wait_recv()
    lax.fori_loop(half - 1, half + 2, near, 0)
    yout[...] = pack(wide[rows:])
    y_copy = remote(yout, yin, y_s, y_r, across)
    y_copy.start()
    y_copy.wait_recv()
    bf[0] = pack(wide[:rows]) + yin[...]

    b_copy = remote(bf.at[0], bf.at[1], bs, br, aux, other_pair)
    b_copy.start()

    def swap(h, k):
        return remote(bf.at[h], x4p.at[h, q], xs.at[h, k - 1], xr.at[h, k - 1], mate(k))

    for k in range(1, 4):
        swap(0, k).start()
    x4p[0, q] = bf[0]

    def put(h, value):
        tq[h, :used] = pack(value)

    def piece(u):
        return pl.ds(pl.multiple_of(u * span, 8), span)

    def scatter(h, k):
        to = lax.rem(group + k, far)
        return remote(tq.at[h, piece(to)], rb.at[h, k - 1], rs.at[h, k - 1], rr.at[h, k - 1], distant(k))

    def reduce(h):
        value = tq[h, piece(group)]
        for k in range(1, far):
            scatter(h, k).wait_recv()
            value = value + rb[h, k - 1]
        aq[h, piece(group)] = value / den[h, piece(group)]

    def spread(h, k):
        ref = aq.at[h, piece(group)]
        return remote(ref, ref, cs.at[h, k - 1], cr.at[h, k - 1], distant(k))

    b_copy.wait_recv()
    for k in range(1, 4):
        swap(1, k).start()
    x4p[1, q] = bf[1]
    own_quarter = pl.ds(pl.multiple_of(q * quarter, 8), quarter)

    def sums(h, carry):
        for k in range(1, 4):
            swap(h, k).wait_recv()
        for src in range(4):
            x4[h, src * rows:(src + 1) * rows] = unpack(x4p[h, src])
        xt[h] = x4[h].T
        put(h, dot(xt[h, own_quarter], x4[0], ((1,), (0,))))
        for k in order:
            scatter(h, k).start()
        return carry

    def spreads(h, carry):
        reduce(h)
        for k in order:
            spread(h, k).start()
        return carry

    def densities(h, carry):
        def arrive(k, inner):
            spread(h, k).wait_recv()
            return inner

        lax.fori_loop(1, far, arrive, 0)
        weight = (h + 1).astype(jnp.float32)
        part[...] += dot(weight * xt[h, own_quarter], unpack(aq[h, :used]), ((0,), (0,)))
        return carry

    order = [k for near_k in range(far // 2, 0, -1) for k in (near_k, far - near_k)][1:]
    part[...] = jnp.zeros_like(part)
    lax.fori_loop(0, 2, sums, 0)
    lax.fori_loop(0, 2, spreads, 0)
    lax.fori_loop(0, 2, densities, 0)
    swapped = dot(x4[1], unpack(aq[1, :used]), ((1,), (1,)))
    for g in range(4):
        @pl.when(q == g)
        def _():
            part[:, g * quarter:(g + 1) * quarter] -= swapped

    def give(k):
        return remote(pout.at[k - 1], pin.at[k - 1], ps.at[k - 1], pr.at[k - 1], mate(k))

    def block(k):
        return pack(part[pl.ds(pl.multiple_of(lax.rem(q + k, 4) * rows, 8), rows)])

    def start(k, carry):
        pout[k - 1] = block(k)
        give(k).start()
        return carry

    def finish(k, total):
        give(k).wait_recv()
        return total + pin[k - 1]

    lax.fori_loop(1, 4, start, 0)
    out_ref[:, 0, :] = unpack(lax.fori_loop(1, 4, finish, block(0)))

    for d in range(2):
        for k in range(steps):
            relay(d, k).wait_send()
            side(d, k).wait_send()
    for copy in (m_copy, y_copy, b_copy):
        copy.wait_send()

    def drain_mates(k, carry):
        for h in range(2):
            swap(h, k).wait_send()
        give(k).wait_send()
        return carry

    def drain_far(k, carry):
        for h in range(2):
            scatter(h, k).wait_send()
            spread(h, k).wait_send()
        return carry

    lax.fori_loop(1, 4, drain_mates, 0)
    lax.fori_loop(1, far, drain_far, 0)


def window(nz, mask, integrals, metric_root, occ_energy, virt_energy):
    rows, _, vir = integrals.shape
    half = nz // 2
    far = nz // 2
    quarter = vir // 4
    packed = rows * 5 // 2
    padded = -(-(quarter * 5 // 2) // (8 * far)) * 8 * far
    vm = pl.BlockSpec(memory_space=pltpu.VMEM)
    sm = pl.BlockSpec(memory_space=pltpu.SMEM)
    f32 = jnp.float32
    dma = pltpu.SemaphoreType.DMA
    out = pl.pallas_call(
        functools.partial(kernel, nz, mask),
        out_shape=jax.ShapeDtypeStruct((rows, 1, vir), f32),
        in_specs=[sm, vm, vm, vm],
        out_specs=vm,
        scratch_shapes=[
            pltpu.VMEM((nz, packed, 128), f32),
            pltpu.VMEM(metric_root.shape, f32),
            pltpu.VMEM((nz, 2 * rows, rows), f32),
            pltpu.VMEM((2 * rows, vir), f32),
            pltpu.VMEM((packed, 128), f32),
            pltpu.VMEM((packed, 128), f32),
            pltpu.VMEM((2, 4, packed, 128), f32),
            pltpu.VMEM((2, 4 * rows, vir), f32),
            pltpu.VMEM((2, vir, 4 * rows), f32),
            pltpu.VMEM((2, packed, 128), f32),
            pltpu.VMEM((2, padded, 128), f32),
            pltpu.VMEM((2, far - 1, padded // far, 128), f32),
            pltpu.VMEM((2, padded, 128), f32),
            pltpu.VMEM((2, padded, 128), f32),
            pltpu.VMEM((4 * rows, vir), f32),
            pltpu.VMEM((3, packed, 128), f32),
            pltpu.VMEM((3, packed, 128), f32),
            pltpu.VMEM((vir, 8), f32),
            dma, dma,
            dma, dma,
            dma((2, half // 2)), dma((2, half // 2)),
            dma((2, half // 2)), dma((2, half // 2)),
            dma, dma,
            dma((2, 3)), dma((2, 3)),
            dma((2, far - 1)), dma((2, far - 1)),
            dma((2, far - 1)), dma((2, far - 1)),
            dma((3,)), dma((3,)),
        ],
        compiler_params=pltpu.CompilerParams(collective_id=mask, has_side_effects=True),
    )(
        occ_energy, integrals, metric_root, virt_energy,
    )
    return out


def shards(nz, integrals, metric_root, occ_energy, virt_energy, partner):
    count = lax.axis_size("pair")
    branches = [functools.partial(window, nz, mask) for mask in range(1, count)]
    return lax.switch(partner[0, 0] - 1, branches, integrals, metric_root, occ_energy, virt_energy)


def solution(mesh):
    nz = mesh.shape["aux"] // 2
    in_specs = (P("aux", "pair", None), P("aux", None), P(), P(), P())
    return jax.shard_map(
        functools.partial(shards, nz), mesh=mesh, in_specs=in_specs,
        out_specs=P("aux", "pair", None), check_vma=False,
    )
```

```python
import functools

import jax
import jax.numpy as jnp
from jax import lax
from jax.experimental import pallas as pl
from jax.experimental.pallas import tpu as pltpu
from jax.sharding import PartitionSpec as P

MESH = pl.DeviceIdType.MESH

def flip(index, mask):
    for bit in (1, 2, 4, 8):
        if mask & bit:
            index = index + bit - 2 * bit * ((index // bit) % 2)
    return index


def split(value):
    high = value.astype(jnp.bfloat16)
    return high, (value - high.astype(jnp.float32)).astype(jnp.bfloat16)


def dot(left, right, dims):
    l_high, l_low = split(left)
    r_high, r_low = split(right)
    one = functools.partial(
        lax.dot_general, dimension_numbers=(dims, ((), ())), preferred_element_type=jnp.float32
    )
    return one(l_high, r_high) + (one(l_high, r_low) + one(l_low, r_high))


def pack(value):
    short = value.shape[0] // 2
    tail = jnp.concatenate([value[:short, 256:], value[short:, 256:]], axis=1)
    return jnp.concatenate([value[:, :128], value[:, 128:256], tail], axis=0)


def unpack(value):
    rows = value.shape[0] * 2 // 5
    tail = jnp.concatenate([value[2 * rows:, :64], value[2 * rows:, 64:]], axis=0)
    return jnp.concatenate([value[:rows], value[rows:2 * rows], tail], axis=1)


def kernel(
    nz, mask,
    occ_ref, ints_ref, metric_ref, virt_ref, out_ref,
    tri, tri_rb, tri_aq, tri_den,
    gat, cols, wide, yout, yin, x4p, x4, xt, bf, tq, rb, aq, den, part, part_t, pout, pin, vcol,
    m_s, m_r, h_s, h_r, y_s, y_r, es, er, bs, br, xs, xr, rs, rr, cs, cr, ps, pr,
):
    aux = lax.axis_index("aux")
    pair = lax.axis_index("pair")
    rows, _, vir = ints_ref.shape
    far = nz // 2
    group = aux // 4
    q = aux % 4
    quarter = vir // 4
    used = quarter * 5 // 2
    span = tq.shape[0] // far
    tri_span = tri.shape[0] // far
    side_of = tri.shape[0] // 2

    is0, is1 = (3 - q) // 3, (q % 2) * (1 - q // 2)
    is2, is3 = (q // 2) * (1 - q % 2), q // 3

    def place(i, j):
        corner = is0 * i * (1 - j)
        row = i + 2 * is2 + 2 * j * is3 + 3 * corner
        column = j * (1 - is3) + 2 * (is1 + is2) + 4 * is3 + 4 * corner
        mirrored = is1 + is3 + is0 * (1 - i) * j
        at = lambda n: pl.ds(pl.multiple_of(n * side_of, 8), side_of)
        return at(row), at(column), mirrored
    mate = lambda k: group * 4 + lax.rem(q + k, 4)
    distant = lambda k: lax.rem(group + k, far) * 4 + q

    barrier = pltpu.get_barrier_semaphore()
    def hello(dev_aux, dev_pair):
        pl.semaphore_signal(barrier, inc=1, device_id={"aux": dev_aux, "pair": dev_pair}, device_id_type=MESH)

    def greet(k, carry):
        hello(distant(k), pair)
        return carry

    core = pair % 2
    twin = flip(pair, 1)
    hello(aux, twin)
    for k in range(1, 4):
        hello(mate(k), pair)
    lax.fori_loop(1, far, greet, 0)
    other_pair = flip(pair, mask)
    hello(aux, other_pair)
    pl.semaphore_wait(barrier, 4 + far)

    def remote(src, dst, s, r, dev_aux, dev_pair=None):
        return pltpu.make_async_remote_copy(
            src_ref=src, dst_ref=dst, send_sem=s, recv_sem=r,
            device_id={"aux": dev_aux, "pair": pair if dev_pair is None else dev_pair},
            device_id_type=MESH,
        )

    steps = far // 2
    gat[group] = pack(ints_ref[:, 0, :])

    def relay(d, k):
        ref = gat.at[lax.rem(group - k + far, far) if d == 0 else lax.rem(group + k, far)]
        if k == steps - 1:
            size = gat.shape[1] // 2
            ref = ref.at[pl.ds(d * size, size)]
        return remote(ref, ref, es.at[d, k], er.at[d, k], distant(1) if d == 0 else distant(far - 1))

    for d in range(2):
        relay(d, 0).start()

    pairs = cols.shape[2]

    def choose_columns(n, carry):
        k, v = n // pairs, n % pairs
        their = lax.rem(q + k, 4)
        halves = []
        for h in range(2):
            tile = (2 * v + h) * 2 + their // 2
            both = metric_ref[:, pl.ds(pl.multiple_of(tile * 2 * rows, 2 * rows), 2 * rows)]
            halves.append(jnp.where(their % 2 == 0, both[:, :rows], both[:, rows:]))
        cols[0, k, v] = jnp.concatenate(halves, axis=1)
        return carry

    lax.fori_loop(0, 4 * pairs, choose_columns, 0)

    def bring(k, c):
        v = core * (pairs // 2) + c
        return remote(cols.at[0, k, v], cols.at[1, k, v], m_s.at[k - 1, c], m_r.at[k - 1, c], mate(k))

    def pass_on(k, c):
        ref = cols.at[1, k, core * (pairs // 2) + c]
        return remote(ref, ref, h_s.at[k - 1, c], h_r.at[k - 1, c], aux, twin)

    def mates_do(act):
        def one(k, carry):
            act(k)
            return carry

        lax.fori_loop(1, 4, one, 0)

    def brings(c):
        mates_do(lambda k: bring(k, c).start())

    def passes(c):
        def one(k):
            bring(k, c).wait_recv()
            pass_on(k, c).start()

        mates_do(one)

    brings(0)
    cols[1, 0] = cols[0, 0]
    wide[...] = jnp.zeros_like(wide)
    tq[...] = jnp.zeros_like(tq)
    den[...] = jnp.full(den.shape, -1.0, jnp.float32)
    v_row = virt_ref[...].reshape(1, vir)
    vcol[...] = jnp.broadcast_to(v_row, (8, vir)).T
    own_rows = vcol[pl.ds(pl.multiple_of(q * quarter, 8), quarter), :1]
    own = occ_ref[pair]
    den[:used] = pack(own + occ_ref[other_pair] - own_rows - v_row)

    def tri_dens(i, carry):
        subs = []
        for j in range(2):
            row, column, _ = place(i, j)
            subs.append(own + own - vcol[row, :1] - vcol[column].T[:1])
        tri_den[pl.ds(pl.multiple_of(i * side_of, 8), side_of)] = jnp.concatenate(subs, axis=1)
        return carry

    lax.fori_loop(0, 2, tri_dens, 0)

    for k in range(1, steps):
        for d in range(2):
            relay(d, k - 1).wait_recv()
            relay(d, k).start()
        if k <= pairs // 2:
            passes(k - 1)
        if k < pairs // 2:
            brings(k)
    for c in range(pairs // 2):
        mates_do(lambda k: pass_on(k, c).wait_recv())

    def accumulate(i, carry):
        block = lax.rem(group + i, far)
        both = cols[1, :, block // 2].reshape(4 * rows, 2 * rows)
        chosen = jnp.where(block % 2 == 0, both[:, :rows], both[:, rows:])
        wide[...] += dot(chosen, unpack(gat[block]), ((1,), (0,)))
        return carry

    def in_turn(n, carry):
        @pl.when(n == far - 1)
        def _():
            for d in range(2):
                relay(d, steps - 1).wait_recv()
        return accumulate(steps + 1 + n, carry)

    lax.fori_loop(0, far, in_turn, 0)

    def give_back(k):
        return remote(yout.at[k - 1], yin.at[k - 1], y_s.at[k - 1], y_r.at[k - 1], mate(4 - k))

    def start_back(k, carry):
        yout[k - 1] = pack(wide[pl.ds(pl.multiple_of(k * rows, 8), rows)])
        give_back(k).start()
        return carry

    def finish_back(k, total):
        give_back(k).wait_recv()
        return total + yin[k - 1]

    lax.fori_loop(1, 4, start_back, 0)
    bf[0] = lax.fori_loop(1, 4, finish_back, pack(wide[:rows]))

    b_copy = remote(bf.at[0], bf.at[1], bs, br, aux, other_pair)
    b_copy.start()

    def swap(h, k):
        return remote(bf.at[h], x4p.at[h, q], xs.at[h, k - 1], xr.at[h, k - 1], mate(k))

    mates_do(lambda k: swap(0, k).start())
    x4p[0, q] = bf[0]

    streams = ((tri, tri_rb, tri_aq, tri_den, tri_span), (tq, rb, aq, den, span))

    def piece(h, u):
        size = streams[h][4]
        return pl.ds(pl.multiple_of(u * size, 8), size)

    def scatter(h, k):
        ref = streams[h][0].at[piece(h, lax.rem(group + k, far))]
        return remote(ref, streams[h][1].at[k - 1], rs.at[h, k - 1], rr.at[h, k - 1], distant(k))

    def spread(h, k):
        ref = streams[h][2].at[piece(h, group)]
        return remote(ref, ref, cs.at[h, k - 1], cr.at[h, k - 1], distant(k))

    def send(copy, h):
        def one(n, carry):
            k = far // 2 + (n // 2) * (2 * (n % 2) - 1)
            copy(h, k).start()
            return carry

        lax.fori_loop(1, far, one, 0)

    def reduce(h):
        def add(k, value):
            scatter(h, k).wait_recv()
            return value + streams[h][1][k - 1]

        mine = piece(h, group)
        streams[h][2][mine] = lax.fori_loop(1, far, add, streams[h][0][mine]) / streams[h][3][mine]

    b_copy.wait_recv()
    mates_do(lambda k: swap(1, k).start())
    x4p[1, q] = bf[1]
    own_quarter = pl.ds(pl.multiple_of(q * quarter, 8), quarter)

    def sums(h, carry):
        mates_do(lambda k: swap(h, k).wait_recv())

        def open_up(src, inner):
            x4[h, pl.ds(pl.multiple_of(src * rows, 8), rows)] = unpack(x4p[h, src])
            return inner

        lax.fori_loop(0, 4, open_up, 0)
        xt[h] = x4[h].T

        @pl.when(h == 0)
        def _():
            def blocks(i, inner):
                subs = []
                for j in range(2):
                    row, column, _ = place(i, j)
                    subs.append(dot(xt[0, row], xt[0, column], ((1,), (1,))))
                tri[pl.ds(pl.multiple_of(i * side_of, 8), side_of)] = jnp.concatenate(subs, axis=1)
                return inner

            lax.fori_loop(0, 2, blocks, 0)
            send(scatter, 0)

        @pl.when(h == 1)
        def _():
            tq[:used] = pack(dot(xt[1, own_quarter], x4[0], ((1,), (0,))))
            send(scatter, 1)
        return carry

    def spread_all(h):
        def arrive(k, inner):
            spread(h, k).wait_recv()
            return inner

        lax.fori_loop(1, far, arrive, 0)

    def tri_densities(i, carry):
        for j in range(2):
            row, column, mirrored = place(i, j)
            block = tri_aq[pl.ds(pl.multiple_of(i * side_of, 8), side_of)][:, j * side_of:(j + 1) * side_of]
            part_t[column] += dot(block, xt[0, row], ((0,), (0,)))
            part_t[row] += mirrored.astype(jnp.float32) * dot(block, xt[0, column], ((1,), (0,)))
        return carry

    part_t[...] = jnp.zeros_like(part_t)
    lax.fori_loop(0, 2, sums, 0)
    for h in range(2):
        reduce(h)
        send(spread, h)
    spread_all(0)
    lax.fori_loop(0, 2, tri_densities, 0)
    spread_all(1)
    cross = unpack(aq[:used])
    part_t[...] += dot(cross, 2.0 * xt[1, own_quarter], ((0,), (0,)))
    part_t[own_quarter] -= dot(cross, xt[1], ((1,), (0,)))
    part[...] = part_t[...].T

    def give(k):
        return remote(pout.at[k - 1], pin.at[k - 1], ps.at[k - 1], pr.at[k - 1], mate(k))

    def rows_of(k):
        return pack(part[pl.ds(pl.multiple_of(lax.rem(q + k, 4) * rows, 8), rows)])

    def start(k, carry):
        pout[k - 1] = rows_of(k)
        give(k).start()
        return carry

    def finish(k, total):
        give(k).wait_recv()
        return total + pin[k - 1]

    lax.fori_loop(1, 4, start, 0)
    out_ref[:, 0, :] = unpack(lax.fori_loop(1, 4, finish, rows_of(0)))

    for d in range(2):
        for k in range(steps):
            relay(d, k).wait_send()
    b_copy.wait_send()

    def drain_mates(k, carry):
        for h in range(2):
            swap(h, k).wait_send()
        give(k).wait_send()
        give_back(k).wait_send()
        for c in range(pairs // 2):
            bring(k, c).wait_send()
            pass_on(k, c).wait_send()
        return carry

    def drain_far(k, carry):
        for h in range(2):
            scatter(h, k).wait_send()
            spread(h, k).wait_send()
        return carry

    lax.fori_loop(1, 4, drain_mates, 0)
    lax.fori_loop(1, far, drain_far, 0)


def window(nz, mask, integrals, metric_root, occ_energy, virt_energy):
    rows, _, vir = integrals.shape
    half = nz // 2
    far = nz // 2
    quarter = vir // 4
    packed = rows * 5 // 2
    padded = -(-(quarter * 5 // 2) // (8 * far)) * 8 * far
    vm = pl.BlockSpec(memory_space=pltpu.VMEM)
    sm = pl.BlockSpec(memory_space=pltpu.SMEM)
    f32 = jnp.float32
    dma = pltpu.SemaphoreType.DMA
    out = pl.pallas_call(
        functools.partial(kernel, nz, mask),
        out_shape=jax.ShapeDtypeStruct((rows, 1, vir), f32),
        in_specs=[sm, vm, vm, vm],
        out_specs=vm,
        scratch_shapes=[
            pltpu.VMEM((2 * rows, 128), f32),
            pltpu.VMEM((far - 1, 2 * rows // far, 128), f32),
            pltpu.VMEM((2 * rows, 128), f32),
            pltpu.VMEM((2 * rows, 128), f32),
            pltpu.VMEM((far, packed, 128), f32),
            pltpu.VMEM((2, 4, far // 2, rows, 2 * rows), f32),
            pltpu.VMEM((4 * rows, vir), f32),
            pltpu.VMEM((3, packed, 128), f32),
            pltpu.VMEM((3, packed, 128), f32),
            pltpu.VMEM((2, 4, packed, 128), f32),
            pltpu.VMEM((2, 4 * rows, vir), f32),
            pltpu.VMEM((2, vir, 4 * rows), f32),
            pltpu.VMEM((2, packed, 128), f32),
            pltpu.VMEM((padded, 128), f32),
            pltpu.VMEM((far - 1, padded // far, 128), f32),
            pltpu.VMEM((padded, 128), f32),
            pltpu.VMEM((padded, 128), f32),
            pltpu.VMEM((4 * rows, vir), f32),
            pltpu.VMEM((vir, 4 * rows), f32),
            pltpu.VMEM((3, packed, 128), f32),
            pltpu.VMEM((3, packed, 128), f32),
            pltpu.VMEM((vir, 8), f32),
            dma((3, far // 4)), dma((3, far // 4)),
            dma((3, far // 4)), dma((3, far // 4)),
            dma((3,)), dma((3,)),
            dma((2, far // 2)), dma((2, far // 2)),
            dma, dma,
            dma((2, 3)), dma((2, 3)),
            dma((2, far - 1)), dma((2, far - 1)),
            dma((2, far - 1)), dma((2, far - 1)),
            dma((3,)), dma((3,)),
        ],
        compiler_params=pltpu.CompilerParams(collective_id=mask, has_side_effects=True),
    )(
        occ_energy, integrals, metric_root, virt_energy,
    )
    return out


def shards(nz, integrals, metric_root, occ_energy, virt_energy, partner):
    count = lax.axis_size("pair")
    branches = [functools.partial(window, nz, mask) for mask in range(1, count)]
    return lax.switch(partner[0, 0] - 1, branches, integrals, metric_root, occ_energy, virt_energy)


def solution(mesh):
    nz = mesh.shape["aux"] // 2
    in_specs = (P("aux", "pair", None), P("aux", None), P(), P(), P())
    return jax.shard_map(
        functools.partial(shards, nz), mesh=mesh, in_specs=in_specs,
        out_specs=P("aux", "pair", None), check_vma=False,
    )
```
